256 devices in a mesh: section: 2 (over x_lo), dec: 32 (over x_hi, z, core), row: 4 (over y).
Axes of the slice: x: 4 (x_hi: 2, x_lo: 2; x = x_hi * 2 + x_lo), y: 4, z: 8, core: 2. Of those that a mesh axis runs over, the one named last changes fastest.
Arguments:
- hidden: bfloat16 [64, 4, 16, 8, 5120], P('dec', None, 'row', None, 'section'), may hold values from -12 to 12
- head_weight: bfloat16 [5120, 64], P('section'), may hold values from -0.078125 to 0.078125
- head_bias: float32 [64], replicated, may hold values from -3 to 3
- lat_cache: bfloat16 [64, 2, 32, 16, 16], P('dec', None, 'row'), may hold values from -6 to 6
- mid_cache: bfloat16 [64, 2, 32, 16, 512], P('dec', None, 'row', None, 'section'), may hold values from -6 to 6
- moves: int32 [64], replicated, may hold values from 0 to 63, each once
- span_index: int32 [64], P('dec'), may hold values from 0 to 3
- conv_in_weight: bfloat16 [3, 3, 3, 16, 512], P(None, None, None, None, 'section'), may hold values from -0.3125 to 0.3125
- conv_in_bias: float32 [512], P('section'), may hold values from -3 to 3
- gn_gain: float32 [512], P('section'), may hold values from 0.25 to 1.75
- gn_bias: float32 [512], P('section'), may hold values from -3 to 3
- mid_weight: bfloat16 [3, 3, 3, 512, 512], P(None, None, None, None, 'section'), may hold values from -0.0546875 to 0.0546875
- mid_bias: float32 [512], P('section'), may hold values from -3 to 3
Outputs:
- decoded: bfloat16 [64, 4, 32, 16, 512], P('dec', None, 'row', None, 'section')
- new_lat_cache: bfloat16 [64, 2, 32, 16, 16], P('dec', None, 'row')
- new_mid_cache: bfloat16 [64, 2, 32, 16, 512], P('dec', None, 'row', None, 'section')
The draws below stay inside these ranges and needn't reach their ends.
Inputs may be any that keep to these rules, and one draw needn't show every extreme that they name: moves holds each of the 64 slots once.
All inputs are finite; a program needn't handle non-finite values.
Results may differ from the reference program's by a relative error of at most 0.012.
Values may be sent and summed in bfloat16 or wider, within the bound.
No kernel may reach another device: no remote copies, remote signals or barrier semaphores. Data moves between devices by JAX's collectives and lax.ppermute only.
A program may use at most 128 MiB of HBM per device.

```python
import jax
import jax.numpy as jnp
from jax import lax

D = 5120
CZ = 16
C = 512
GROUPS = 32
F = 4
CACHE = 2
W = 16
STREAMS = 64
H = 32
HP = 16
WP = 8
PO = 64


def draw_hidden(key, part):
    shape = (STREAMS, F, HP, WP, D)
    position = jnp.arange(HP, dtype=jnp.float32) / (HP - 1)
    base = jax.random.truncated_normal(key, -6.0, 6.0, shape, jnp.float32)
    scale = jnp.exp(jnp.log(0.5) + position * jnp.log(4.0))
    return (base * scale[None, None, :, None, None]).astype(jnp.bfloat16)


def plant(drawn, key, least, largest):
    spot = [jax.random.randint(jax.random.fold_in(key, axis), (), 0, length) for axis, length in enumerate(drawn.shape)]
    main_axis = drawn.shape.index(max(drawn.shape))
    beside = spot[:main_axis] + [(spot[main_axis] + 1) % drawn.shape[main_axis]] + spot[main_axis + 1:]
    return drawn.at[tuple(spot)].set(least).at[tuple(beside)].set(largest)


def level_of(key, shape, shards, smallest, largest):
    level = 1.0
    for dim, shards_of in shards:
        heights = jax.random.uniform(jax.random.fold_in(jax.random.fold_in(key, 6), dim), (shards_of,), jnp.float32, smallest / len(shards), largest / len(shards))
        level = level * jnp.repeat(jnp.exp(heights), shape[dim] // shards_of).reshape((-1,) + (1,) * (len(shape) - 1 - dim))
    return level


def noise(rng, extent, spread, bound, split=(), kind=jnp.bfloat16):
    factor_of = level_of(rng, extent, split, -0.22, 0.18) if split else 1.0
    result = jax.random.normal(rng, extent, jnp.float32) * spread * factor_of
    return jnp.minimum(jnp.maximum(result, -bound), bound).astype(kind)


def setup_inputs(seed: int = 0) -> dict:
    arg_keys = jax.random.split(jax.random.key(seed), 14)
    hidden = draw_hidden(jax.random.fold_in(arg_keys[13], 71), 0)
    head_weight = noise(arg_keys[1], (D, PO), D ** -0.5, 0.078125, ((0, 2),))
    head_bias = noise(arg_keys[2], (PO,), 0.5, 3.0, (), jnp.float32)
    lat_cache = noise(arg_keys[3], (STREAMS, CACHE, H, W, CZ), 1.0, 6.0, ((0, 32), (2, 4)))
    mid_cache = noise(arg_keys[4], (STREAMS, CACHE, H, W, C), 1.0, 6.0, ((0, 32), (2, 4), (4, 2)))
    moves = jax.random.permutation(arg_keys[5], STREAMS).astype(jnp.int32)
    span_index = plant(jax.random.randint(arg_keys[6], (STREAMS,), 0, 4), jax.random.fold_in(arg_keys[6], 1), 0, 3).astype(jnp.int32)
    conv_in_weight = noise(arg_keys[7], (3, 3, 3, CZ, C), (27 * CZ) ** -0.5, 0.3125, ((4, 2),))
    conv_in_bias = noise(arg_keys[8], (C,), 0.5, 3.0, ((0, 2),), jnp.float32)
    gn_gain = jnp.clip(1.0 + 0.15 * jax.random.normal(arg_keys[9], (C,), jnp.float32), 0.25, 1.75)
    gn_bias = noise(arg_keys[10], (C,), 0.5, 3.0, ((0, 2),), jnp.float32)
    mid_weight = noise(arg_keys[11], (3, 3, 3, C, C), (27 * C) ** -0.5, 0.0546875, ((4, 2),))
    mid_bias = noise(arg_keys[12], (C,), 0.5, 3.0, ((0, 2),), jnp.float32)
    return dict(hidden=hidden, head_weight=head_weight, head_bias=head_bias, lat_cache=lat_cache, mid_cache=mid_cache, moves=moves, span_index=span_index, conv_in_weight=conv_in_weight, conv_in_bias=conv_in_bias, gn_gain=gn_gain, gn_bias=gn_bias, mid_weight=mid_weight, mid_bias=mid_bias)


def conv_taps(padded, weight, frames, rows, cols):
    cin = padded.shape[-1]
    total = jnp.zeros((frames * rows * cols, weight.shape[-1]), jnp.float32)
    for a in range(3):
        for b in range(3):
            for e in range(3):
                tap = padded[a:a + frames, b:b + rows, e:e + cols].reshape(-1, cin)
                total = total + jnp.dot(tap, weight[a, b, e], preferred_element_type=jnp.float32)
    return total.reshape(frames, rows, cols, -1)

def reference(hidden, head_weight, head_bias, lat_cache, mid_cache, moves, span_index, conv_in_weight, conv_in_bias, gn_gain, gn_bias, mid_weight, mid_bias):
    streams, frames, half_rows, half_cols, width = hidden.shape
    patches = jnp.dot(hidden.reshape(-1, width), head_weight, preferred_element_type=jnp.float32) + head_bias
    latent = patches.reshape(streams, frames, half_rows, half_cols, 2, 2, CZ)
    latent = latent.transpose(0, 1, 2, 4, 3, 5, 6).reshape(streams, frames, 2 * half_rows, 2 * half_cols, CZ).astype(jnp.bfloat16)
    live = (span_index > 0).astype(jnp.bfloat16)[:, None, None, None, None]
    prev_lat = jnp.take(lat_cache, moves.astype(jnp.int32), axis=0) * live
    prev_mid = jnp.take(mid_cache, moves.astype(jnp.int32), axis=0) * live

    def decode_one(items):
        lat_prev, lat_now, mid_prev = items
        x_in = jnp.concatenate([lat_prev, lat_now], 0)
        x_pad = jnp.pad(x_in, ((0, 0), (1, 1), (1, 1), (0, 0)))
        first = (conv_taps(x_pad, conv_in_weight, F, H, W) + conv_in_bias).astype(jnp.bfloat16)
        grouped = first.astype(jnp.float32).reshape(F, H, W, GROUPS, C // GROUPS)
        gmean = lax.optimization_barrier(jnp.mean(grouped, axis=(0, 1, 2, 4), keepdims=True))
        gvar = lax.optimization_barrier(jnp.mean(grouped * grouped, axis=(0, 1, 2, 4), keepdims=True)) - gmean * gmean
        scaled = ((grouped - gmean) * lax.rsqrt(gvar + 1e-05)).reshape(F, H, W, C) * gn_gain + gn_bias
        act = jax.nn.silu(scaled).astype(jnp.bfloat16)
        m_in = jnp.concatenate([mid_prev, act], 0)
        m_pad = jnp.pad(m_in, ((0, 0), (1, 1), (1, 1), (0, 0)))
        conv = conv_taps(m_pad, mid_weight, F, H, W) + mid_bias
        out = (first.astype(jnp.float32) + conv).astype(jnp.bfloat16)
        return (out, act[F - CACHE:])
    decoded, new_mid = lax.map(decode_one, (prev_lat, latent, prev_mid))
    return (decoded, latent[:, F - CACHE:], new_mid)
```

```python
import jax
import jax.numpy as jnp
from jax import lax
from jax.experimental import pallas as pl
from jax.experimental.pallas import tpu as pltpu
from jax.sharding import PartitionSpec as P

CZ = 16
C = 512
GROUPS = 32
CACHE = 2
SWAP = [(0, 1), (1, 0)]
VMEM = pl.BlockSpec(memory_space=pltpu.VMEM)
SMEM = pl.BlockSpec(memory_space=pltpu.SMEM)


def neighbours(block, width):
    count = lax.axis_size("row")
    down = [(i, i + 1) for i in range(count - 1)]
    up = [(i + 1, i) for i in range(count - 1)]
    low = lax.ppermute(block[:, :, -width:], "row", down)
    high = lax.ppermute(block[:, :, :width], "row", up)
    return low, high


def pick_kernel(me_ref, moves_ref, got_ref, twin_ref, send_ref, lat_ref):
    dec = me_ref[0]
    core = dec % 2
    hosts = got_ref.shape[0]

    def place(slot, offset, rows, write):
        host = slot // 4
        mine = (slot // 2) % 2 == core
        start = pl.multiple_of(offset + (slot % 2) * rows, 8)

        @pl.when(mine)
        def _():
            write(got_ref[host, pl.ds(start, rows), :])

        @pl.when(jnp.logical_not(mine))
        def _():
            write(twin_ref[host, pl.ds(start, rows), :])

    for host in range(hosts):
        for k in range(2):
            slot = moves_ref[4 * host + 2 * core + k]

            def write(value, host=host, k=k):
                for side in range(2):
                    send_ref[side * hosts + host, k * 16 : (k + 1) * 16, :] = value

            place(slot, 0, 16, write)
    for k in range(2):
        slot = moves_ref[2 * dec + k]

        def write_lat(value, k=k):
            lat_ref[k] = value

        place(slot, 32, 8, write_lat)


def shards(
    hidden,
    head_weight,
    head_bias,
    lat_cache,
    mid_cache,
    moves,
    span_index,
    conv_in_weight,
    conv_in_bias,
    gn_gain,
    gn_bias,
    mid_weight,
    mid_bias,
):
    streams, frames, half_rows, half_cols, width_part = hidden.shape
    rows, cols = 2 * half_rows, 2 * half_cols
    part = conv_in_weight.shape[-1]
    section = lax.axis_index("section")
    dec = lax.axis_index("dec")
    row = lax.axis_index("row")
    hosts = lax.axis_size("dec") // 2

    mid_pieces = mid_cache.transpose(1, 2, 0, 3, 4).reshape(hosts, streams * cols, part)
    lat_half = lax.dynamic_index_in_dim(lat_cache, section, 1, keepdims=False)
    lat_half = lat_half.reshape(1, streams * rows, cols * CZ)
    send = jnp.concatenate(
        [mid_pieces, jnp.broadcast_to(lat_half, (hosts,) + lat_half.shape[1:])], axis=1
    )
    spread = [[2 * j + c for j in range(hosts)] for c in range(2)]
    got = lax.all_to_all(send, "dec", 0, 0, axis_index_groups=spread)
    twin = lax.ppermute(got, "dec", [(i, i ^ 1) for i in range(2 * hosts)])
    me = jnp.stack([dec, section, row]).astype(jnp.int32)
    back, lat_pick = pl.pallas_call(
        pick_kernel,
        out_shape=(
            jax.ShapeDtypeStruct((2 * hosts, streams * cols, part), jnp.bfloat16),
            jax.ShapeDtypeStruct((streams, rows, cols * CZ), jnp.bfloat16),
        ),
        in_specs=[SMEM, SMEM, VMEM, VMEM],
        out_specs=(VMEM, VMEM),
        name="pick",
    )(me, moves, got, twin)
    gather = [
        [s * 2 * hosts + 2 * j + c for s in range(2) for j in range(hosts)] for c in range(2)
    ]
    pieces = lax.all_to_all(back, ("section", "dec"), 0, 0, axis_index_groups=gather)
    live = (span_index > 0).astype(jnp.bfloat16)[:, None, None, None, None]
    prev_mid = pieces.reshape(2, CACHE, rows, streams, cols, part)
    prev_mid = prev_mid.transpose(3, 1, 2, 4, 0, 5).reshape(streams, CACHE, rows, cols, 2 * part)
    prev_mid = prev_mid * live

    def whole(own):
        other = lax.ppermute(own, "section", SWAP)
        return jnp.where(
            section == 0,
            jnp.concatenate([own, other], -1),
            jnp.concatenate([other, own], -1),
        )

    in_weight = whole(conv_in_weight.reshape(27 * CZ, part)).reshape(3, 3, 3, CZ, 2 * part)
    vectors = whole(jnp.stack([conv_in_bias, gn_gain, gn_bias]))

    partial = jnp.dot(
        hidden.reshape(-1, width_part), head_weight, preferred_element_type=jnp.float32
    )
    patches = partial + lax.ppermute(partial, "section", SWAP) + head_bias
    latent = patches.reshape(streams, frames, half_rows, half_cols, 2, 2, CZ)
    latent = (
        latent.transpose(0, 1, 2, 4, 3, 5, 6)
        .reshape(streams, frames, rows, cols * CZ)
        .astype(jnp.bfloat16)
    )

    lat_other = lax.ppermute(lat_pick, "section", SWAP)
    prev_lat = jnp.where(
        section == 0, jnp.stack([lat_pick, lat_other], 1), jnp.stack([lat_other, lat_pick], 1)
    )
    prev_lat = prev_lat * live[..., 0]
    x_in = jnp.concatenate([prev_lat, latent], 1)
    low, high = neighbours(x_in, 2)
    x_rim = jnp.concatenate([low, x_in, high], 2).reshape(
        streams, CACHE + frames, rows + 4, cols, CZ
    )
    dims = ("NDHWC", "DHWIO", "NDHWC")
    window = (1, 1, 1)
    sides = ((0, 0), (0, 0), (1, 1))
    first = lax.conv_general_dilated(
        x_rim, in_weight, window, sides, dimension_numbers=dims, preferred_element_type=jnp.float32
    )
    first = (first + vectors[0]).astype(jnp.bfloat16)
    own = first[:, :, 1:-1].astype(jnp.float32).reshape(streams, frames * rows * cols, 2 * part)
    size = C // GROUPS
    sums = jnp.stack([jnp.sum(own, 1), jnp.sum(own * own, 1)])
    sums = sums.reshape(2, streams, GROUPS, size).sum(-1)
    bands = lax.axis_size("row")
    total = sums
    for shift in range(1, bands):
        total = total + lax.ppermute(sums, "row", [(i, (i + shift) % bands) for i in range(bands)])
    count = frames * rows * bands * cols * size
    mean = total[0] / count
    variance = total[1] / count - mean * mean
    spread_out = lambda v: jnp.repeat(v, size, axis=-1)[:, None, None, None, :]
    scaled = (first.astype(jnp.float32) - spread_out(mean)) * spread_out(lax.rsqrt(variance + 1e-05))
    act = jax.nn.silu(scaled * vectors[1] + vectors[2])
    line = row * rows - 1 + lax.iota(jnp.int32, rows + 2)
    inside = (line >= 0) & (line < rows * bands)
    act = jnp.where(inside[None, None, :, None, None], act, 0.0).astype(jnp.bfloat16)

    low, high = neighbours(prev_mid, 1)
    prev_rim = jnp.concatenate([low, prev_mid, high], 2)
    m_in = jnp.concatenate([prev_rim, act], 1)
    conv = lax.conv_general_dilated(
        m_in, mid_weight, window, sides, dimension_numbers=dims, preferred_element_type=jnp.float32
    )
    start = section * part
    own_first = lax.dynamic_slice_in_dim(first[:, :, 1:-1], start, part, 4)
    decoded = (own_first.astype(jnp.float32) + conv + mid_bias).astype(jnp.bfloat16)
    new_mid = lax.dynamic_slice_in_dim(act[:, frames - CACHE :, 1:-1], start, part, 4)
    new_lat = latent[:, frames - CACHE :].reshape(streams, CACHE, rows, cols, CZ)
    return (decoded, new_lat, new_mid)


def solution(mesh):
    placed = (
        P("dec", None, "row", None, "section"),
        P("section", None),
        P(),
        P("dec", None, "row", None, None),
        P("dec", None, "row", None, "section"),
        P(),
        P("dec"),
        P(None, None, None, None, "section"),
        P("section"),
        P("section"),
        P("section"),
        P(None, None, None, None, "section"),
        P("section"),
    )
    return jax.shard_map(
        shards,
        mesh=mesh,
        in_specs=placed,
        out_specs=(
            P("dec", None, "row", None, "section"),
            P("dec", None, "row", None, None),
            P("dec", None, "row", None, "section"),
        ),
        check_vma=False,
    )
```

```python
import functools

import jax
import jax.numpy as jnp
from jax import lax
from jax.experimental import pallas as pl
from jax.experimental.pallas import tpu as pltpu
from jax.sharding import PartitionSpec as P

CZ = 16
C = 512
GROUPS = 32
CACHE = 2
SWAP = [(0, 1), (1, 0)]
VMEM = pl.BlockSpec(memory_space=pltpu.VMEM)
SMEM = pl.BlockSpec(memory_space=pltpu.SMEM)
ANY = pl.BlockSpec(memory_space=pl.ANY)
F32 = jnp.float32
BF16 = jnp.bfloat16


def call(kernel, name, out_shape, in_specs, out_specs=None, scratch=(), aliases=None, limit=48):
    return pl.pallas_call(
        kernel,
        out_shape=out_shape,
        in_specs=in_specs,
        out_specs=VMEM if out_specs is None else out_specs,
        scratch_shapes=scratch,
        input_output_aliases=aliases or {},
        compiler_params=pltpu.CompilerParams(vmem_limit_bytes=limit << 20),
        name=name,
    )


def head_kernel(hidden_ref, weight_ref, out_ref):
    product = jnp.dot(hidden_ref[...], weight_ref[...], preferred_element_type=F32)
    for frame in range(out_ref.shape[0]):
        for q in range(2):
            parts = [
                product[(frame * 4 + i) * 8 : (frame * 4 + i + 1) * 8, q * 32 : (q + 1) * 32]
                for i in range(4)
            ]
            out_ref[frame, pl.ds(q, 8, stride=2), :] = jnp.concatenate(parts, axis=1)


def pack_kernel(lat_ref, mid_ref, out_ref):
    both = []
    for frame in range(2):
        rows = [lat_ref[k, frame, r] for k in range(2) for r in range(8)]
        both.append(jnp.concatenate(rows, axis=1))
    for piece in range(16):
        frame, row = divmod(piece, 8)
        for k in range(2):
            out_ref[piece, k * 16 : (k + 1) * 16, :] = mid_ref[k, frame, row]
        for frame in range(2):
            out_ref[piece, 32 + frame * 16 : 48 + frame * 16, :] = both[frame]


def pick_kernel(
    me_ref, moves_ref, span_ref, got_ref, twin_ref, part_ref, rest_ref, bias_ref, send_ref, x_ref
):
    dec = me_ref[0]
    core = dec % 2
    hosts = got_ref.shape[0]

    def place(slot, write):
        mine = (slot // 2) % 2 == core

        @pl.when(mine)
        def _():
            write(got_ref, slot // 4, slot % 2)

        @pl.when(jnp.logical_not(mine))
        def _():
            write(twin_ref, slot // 4, slot % 2)

    for host in range(hosts):
        for k in range(2):

            def write(ref, source, which, host=host, k=k):
                value = ref[source, pl.ds(pl.multiple_of(which * 16, 16), 16), :]
                for side in range(2):
                    send_ref[side * hosts + host, k * 16 : (k + 1) * 16, :] = value

            place(moves_ref[4 * host + 2 * core + k], write)
    for k in range(2):
        live = (span_ref[k] > 0).astype(F32)

        def write_lat(ref, source, which, k=k, live=live):
            for frame in range(2):
                lat = ref[
                    source,
                    32 + frame * 16 : 48 + frame * 16,
                    pl.ds(pl.multiple_of(which * 128, 128), 128),
                ]
                x_ref[k, frame] = (lat.astype(F32) * live).astype(BF16)

        place(moves_ref[2 * dec + k], write_lat)
        for f in range(4):
            latent = part_ref[k * 4 + f] + rest_ref[k * 4 + f] + bias_ref[...]
            x_ref[k, 2 + f] = latent.astype(BF16)


def shifted(value, step):
    line = lax.broadcasted_iota(jnp.int32, value.shape, 0)
    edge = 0 if step == 1 else value.shape[0] - 1
    moved = pltpu.roll(value, step % value.shape[0], axis=0)
    return jnp.where(line == edge, 0.0, moved)


def first_kernel(x_ref, low_ref, high_ref, weight_ref, bias_ref, first_ref, stats_ref, lat_ref, taps):
    taps[...] = jnp.zeros_like(taps)

    def fill(index, _):
        k, f = index // 6, index % 6
        wide = jnp.concatenate(
            [low_ref[k, f][:, 96:], x_ref[k, f], high_ref[k, f][:, :32]], axis=1
        ).astype(F32)
        for e, value in enumerate((shifted(wide, 1), wide, shifted(wide, -1))):
            value = value.astype(BF16)
            for r in range(10):
                taps[index, r, :, e * 48 : (e + 1) * 48] = value[:, 16 * r : 16 * r + 48]
        return 0

    lax.fori_loop(0, 12, fill, 0)
    for k in range(2):
        total = jnp.zeros((640, C), F32) + bias_ref[...]
        for a in range(3):
            total = total + jnp.dot(
                taps[k * 6 + a : k * 6 + a + 4].reshape(640, 256),
                weight_ref[a],
                preferred_element_type=F32,
            )
        rounded = total.astype(BF16).reshape(4, 10, 16, C)
        first_ref[k] = rounded
        own = rounded[:, 1:9].reshape(512, C).astype(F32)
        stats_ref[k : k + 1, :] = jnp.sum(own, 0, keepdims=True)
        stats_ref[2 + k : 3 + k, :] = jnp.sum(own * own, 0, keepdims=True)
        for f in range(2):
            for r in range(8):
                lat_ref[k, f, r] = x_ref[k, 4 + f][:, 16 * r : 16 * r + 16]


def group_sum(value):
    lane = lax.broadcasted_iota(jnp.int32, value.shape, 1)
    size = value.shape[1]
    for step in (1, 2, 4, 8):
        ahead = pltpu.roll(value, size - step, axis=1)
        behind = pltpu.roll(value, step, axis=1)
        value = value + jnp.where((lane // step) % 2 == 0, ahead, behind)
    return value


def spread_taps(taps, index, row, value):
    width = value.shape[1]
    for e, moved in enumerate((shifted(value, 1), value, shifted(value, -1))):
        taps[index, row, :, e * width : (e + 1) * width] = moved.astype(BF16)


def block_kernel(
    count,
    me_ref,
    first_ref,
    own_ref,
    near_ref,
    far_ref,
    back_ref,
    vectors_ref,
    bias_ref,
    weight_ref,
    decoded_ref,
    early_ref,
    cache_ref,
    taps,
    weight,
    total,
    sems,
):
    section, row = me_ref[1], me_ref[2]
    copies = [
        pltpu.make_async_copy(weight_ref.at[i], weight.at[i], sems.at[i]) for i in range(9)
    ]
    for copy in copies:
        copy.start()
    sums = group_sum(own_ref[...] + near_ref[...] + far_ref[...] + back_ref[...]) / count
    mean = sums[0:2]
    scale = lax.rsqrt(sums[2:4] - mean * mean + 1e-05) * vectors_ref[1:2]
    for k in range(2):
        centre, factor = mean[k : k + 1], scale[k : k + 1]

        def fill(index, _):
            f, r = index // 10, index % 10
            value = (first_ref[k, f, r].astype(F32) - centre) * factor + vectors_ref[2:3]
            value = 0.5 * value * (1.0 + jnp.tanh(0.5 * value))
            line = row * 8 + r - 1
            value = jnp.where((line >= 0) & (line < 32), value, 0.0)
            spread_taps(taps, k * 4 + f, r, value)
            return 0

        lax.fori_loop(0, 40, fill, 0, unroll=2)
    start = pl.multiple_of(section * 256, 256)
    for k in range(2):
        for t in range(4):
            total[k * 4 + t] = (
                first_ref[k, t, 1:9, :, pl.ds(start, 256)].astype(F32).reshape(128, 256)
                + bias_ref[...]
            )
        for f in range(2):
            cache_ref[k, f] = taps[k * 4 + 2 + f, 1:9, :, pl.ds(C + start, 256)]
    for a in range(3):
        frames = 2 + a
        for b in range(3):
            copies[a * 3 + b].wait()
            for k in range(2):
                lhs = taps[k * 4 : k * 4 + frames, b : b + 8].reshape(frames * 128, 3 * C)
                part = jnp.dot(lhs, weight[a * 3 + b], preferred_element_type=F32)
                total[k * 4 + 2 - a : k * 4 + 4] += part.reshape(frames, 128, 256)
    for k in range(2):
        early_ref[k] = total[k * 4 : k * 4 + 2]
        for t in range(2, 4):
            decoded_ref[k, t] = total[k * 4 + t].astype(BF16).reshape(8, 16, 256)


def cache_kernel(
    span_ref,
    pieces_ref,
    low_ref,
    high_ref,
    early_ref,
    weight_ref,
    decoded_ref,
    out_ref,
    taps,
    weight,
    total,
    rounded,
    sems,
    done,
):
    copies = [
        pltpu.make_async_copy(weight_ref.at[i], weight.at[i], sems.at[i]) for i in range(6)
    ]
    for copy in copies:
        copy.start()
    for k in range(2):
        live = (span_ref[k] > 0).astype(F32)
        rows = slice(k * 16, k * 16 + 16)

        def put(frame, r, left, right):
            value = jnp.concatenate([left, right], axis=1).astype(F32) * live
            spread_taps(taps, k * 2 + frame, r, value)

        for frame in range(2):
            put(frame, 0, low_ref[0, frame, rows], low_ref[1, frame, rows])
            put(frame, 9, high_ref[0, frame, rows], high_ref[1, frame, rows])

        def fill(index, _):
            frame, r = index // 8, index % 8
            put(frame, r + 1, pieces_ref[index, rows], pieces_ref[16 + index, rows])
            return 0

        lax.fori_loop(0, 16, fill, 0, unroll=2)
    total[...] = early_ref[...].reshape(total.shape)
    for a in range(2):
        frames = 2 - a
        for b in range(3):
            copies[a * 3 + b].wait()
            for k in range(2):
                lhs = taps[k * 2 + a : k * 2 + 2, b : b + 8].reshape(frames * 128, 3 * C)
                part = jnp.dot(lhs, weight[a * 3 + b], preferred_element_type=F32)
                total[k * 2 : k * 2 + frames] += part.reshape(frames, 128, 256)
    outs = []
    for k in range(2):
        rounded[k] = total[k * 2 : k * 2 + 2].astype(BF16).reshape(2, 8, 16, 256)
        outs.append(pltpu.make_async_copy(rounded.at[k], out_ref.at[k, pl.ds(0, 2)], done.at[k]))
        outs[k].start()
    for copy in outs:
        copy.wait()


def beside(block):
    count = lax.axis_size("row")
    down = [(i, i + 1) for i in range(count - 1)]
    up = [(i + 1, i) for i in range(count - 1)]
    return down, up


def shards(
    hidden,
    head_weight,
    head_bias,
    lat_cache,
    mid_cache,
    moves,
    span_index,
    conv_in_weight,
    conv_in_bias,
    gn_gain,
    gn_bias,
    mid_weight,
    mid_bias,
):
    streams, frames, half_rows, half_cols, width_part = hidden.shape
    rows, cols = 2 * half_rows, 2 * half_cols
    part = conv_in_weight.shape[-1]
    section = lax.axis_index("section")
    dec = lax.axis_index("dec")
    row = lax.axis_index("row")
    bands = lax.axis_size("row")
    hosts = lax.axis_size("dec") // 2
    down, up = beside(None)
    shape = jax.ShapeDtypeStruct
    me = jnp.stack([dec, section, row]).astype(jnp.int32)

    send = call(
        pack_kernel, "pack", shape((hosts, 64, part), BF16), [VMEM, VMEM]
    )(lat_cache, mid_cache)
    spread = [[2 * j + c for j in range(hosts)] for c in range(2)]
    got = lax.all_to_all(send, "dec", 0, 0, axis_index_groups=spread)
    def whole(own):
        other = lax.ppermute(own, "section", SWAP)
        return jnp.where(
            section == 0,
            jnp.concatenate([own, other], -1),
            jnp.concatenate([other, own], -1),
        )

    in_weight = whole(conv_in_weight.transpose(0, 2, 1, 3, 4).reshape(3, 9 * CZ, part))
    in_weight = jnp.pad(in_weight, ((0, 0), (0, 256 - 9 * CZ), (0, 0)))
    vectors = whole(jnp.stack([conv_in_bias, gn_gain, gn_bias]))

    columns = head_weight.reshape(width_part, 2, 2, CZ).transpose(0, 2, 1, 3).reshape(width_part, -1)
    bias = head_bias.reshape(2, 2, CZ).transpose(1, 0, 2).reshape(1, 2, 1, 2 * CZ)
    bias = jnp.broadcast_to(bias, (half_cols, 2, half_rows, 2 * CZ)).reshape(cols, rows * CZ)
    partial = call(
        head_kernel, "head", shape((streams * frames, cols, rows * CZ), F32), [VMEM, VMEM]
    )(hidden.reshape(-1, width_part), columns)
    rest = lax.ppermute(partial, "section", SWAP)

    got, rest, in_weight, vectors = lax.optimization_barrier((got, rest, in_weight, vectors))
    twin = lax.ppermute(got, "dec", [(i, i ^ 1) for i in range(2 * hosts)])
    back, x_in = call(
        pick_kernel,
        "pick",
        (
            shape((2 * hosts, 32, part), BF16),
            shape((streams, CACHE + frames, cols, rows * CZ), BF16),
        ),
        [SMEM, SMEM, SMEM] + [VMEM] * 5,
        (VMEM, VMEM),
    )(me, moves, span_index, got, twin, partial, rest, bias)
    gather = [
        [s * 2 * hosts + 2 * j + c for s in range(2) for j in range(hosts)] for c in range(2)
    ]
    pieces = lax.all_to_all(back, ("section", "dec"), 0, 0, axis_index_groups=gather)

    low = lax.ppermute(x_in, "row", down)
    high = lax.ppermute(x_in, "row", up)
    first, stats, new_lat = call(
        first_kernel,
        "first",
        (
            shape((streams, frames, rows + 2, cols, 2 * part), BF16),
            shape((4, 2 * part), F32),
            shape((streams, CACHE, rows, cols, CZ), BF16),
        ),
        [VMEM] * 5,
        (VMEM, VMEM, VMEM),
        [pltpu.VMEM((streams * (CACHE + frames), rows + 2, cols, 256), BF16)],
    )(x_in, low, high, in_weight, vectors[0:1])
    others = [
        lax.ppermute(stats, "row", [(i, (i + shift) % bands) for i in range(bands)])
        for shift in range(1, bands)
    ]
    pieces, new_lat = lax.optimization_barrier((pieces, new_lat))
    edges = pieces.reshape(2, CACHE, rows, 32, part)
    low_mid = lax.ppermute(edges[:, :, rows - 1], "row", down)
    others, edge = lax.optimization_barrier((others, edges[:, :, 0]))
    high_mid = lax.ppermute(edge, "row", up)
    taps_weight = mid_weight.reshape(9, 3 * 2 * part, part)
    count = float(frames * rows * bands * cols * (C // GROUPS))
    decoded, early, new_mid = call(
        functools.partial(block_kernel, count),
        "block",
        (
            shape((streams, frames, rows, cols, part), BF16),
            shape((streams, CACHE, rows * cols, part), F32),
            shape((streams, CACHE, rows, cols, part), BF16),
        ),
        [SMEM] + [VMEM] * 7 + [ANY],
        (VMEM, VMEM, VMEM),
        [
            pltpu.VMEM((streams * frames, rows + 2, cols, 3 * 2 * part), BF16),
            pltpu.VMEM((9, 3 * 2 * part, part), BF16),
            pltpu.VMEM((streams * frames, rows * cols, part), F32),
            pltpu.SemaphoreType.DMA((9,)),
        ],
    )(me, first, stats, *others, vectors, mid_bias.reshape(1, part), taps_weight)

    decoded = call(
        cache_kernel,
        "cache",
        shape(decoded.shape, BF16),
        [SMEM] + [VMEM] * 4 + [ANY, ANY],
        ANY,
        [
            pltpu.VMEM((streams * CACHE, rows + 2, cols, 3 * 2 * part), BF16),
            pltpu.VMEM((6, 3 * 2 * part, part), BF16),
            pltpu.VMEM((streams * CACHE, rows * cols, part), F32),
            pltpu.VMEM((streams, CACHE, rows, cols, part), BF16),
            pltpu.SemaphoreType.DMA((6,)),
            pltpu.SemaphoreType.DMA((2,)),
        ],
        {6: 0},
    )(span_index, pieces, low_mid, high_mid, early, taps_weight, decoded)
    return (decoded, new_lat, new_mid)


def solution(mesh):
    placed = (
        P("dec", None, "row", None, "section"),
        P("section", None),
        P(),
        P("dec", None, "row", None, None),
        P("dec", None, "row", None, "section"),
        P(),
        P("dec"),
        P(None, None, None, None, "section"),
        P("section"),
        P("section"),
        P("section"),
        P(None, None, None, None, "section"),
        P("section"),
    )
    return jax.shard_map(
        shards,
        mesh=mesh,
        in_specs=placed,
        out_specs=(
            P("dec", None, "row", None, "section"),
            P("dec", None, "row", None, None),
            P("dec", None, "row", None, "section"),
        ),
        check_vma=False,
    )
```

```python
import functools

import jax
import jax.numpy as jnp
from jax import lax
from jax.experimental import pallas as pl
from jax.experimental.pallas import tpu as pltpu
from jax.sharding import PartitionSpec as P

CZ = 16
C = 512
GROUPS = 32
CACHE = 2
SWAP = [(0, 1), (1, 0)]
VMEM = pl.BlockSpec(memory_space=pltpu.VMEM)
SMEM = pl.BlockSpec(memory_space=pltpu.SMEM)
ANY = pl.BlockSpec(memory_space=pl.ANY)
F32 = jnp.float32
BF16 = jnp.bfloat16


def call(kernel, name, out_shape, in_specs, out_specs=None, scratch=(), aliases=None, limit=48):
    return pl.pallas_call(
        kernel,
        out_shape=out_shape,
        in_specs=in_specs,
        out_specs=VMEM if out_specs is None else out_specs,
        scratch_shapes=scratch,
        input_output_aliases=aliases or {},
        compiler_params=pltpu.CompilerParams(vmem_limit_bytes=limit << 20),
        name=name,
    )


def head_kernel(hidden_ref, weight_ref, out_ref):
    product = jnp.dot(hidden_ref[...], weight_ref[...], preferred_element_type=F32)
    for frame in range(out_ref.shape[0]):
        for q in range(2):
            parts = [
                product[(frame * 4 + i) * 8 : (frame * 4 + i + 1) * 8, q * 32 : (q + 1) * 32]
                for i in range(4)
            ]
            out_ref[frame, pl.ds(q, 8, stride=2), :] = jnp.concatenate(parts, axis=1)


def pack_kernel(lat_ref, mid_ref, out_ref):
    both = []
    for frame in range(2):
        rows = [lat_ref[k, frame, r] for k in range(2) for r in range(8)]
        both.append(jnp.concatenate(rows, axis=1))
    for piece in range(16):
        frame, row = divmod(piece, 8)
        for k in range(2):
            out_ref[piece, k * 16 : (k + 1) * 16, :] = mid_ref[k, frame, row]
        for frame in range(2):
            out_ref[piece, 32 + frame * 16 : 48 + frame * 16, :] = both[frame]


def pick_kernel(
    me_ref, moves_ref, span_ref, got_ref, twin_ref, part_ref, rest_ref, bias_ref, send_ref, x_ref
):
    dec = me_ref[0]
    core = dec % 2
    hosts = got_ref.shape[0]

    def find(slot, rows, lanes):
        mine = (slot // 2) % 2 == core
        source = slot // 4
        return jnp.where(mine, got_ref[source, rows, lanes], twin_ref[source, rows, lanes])

    every = slice(0, got_ref.shape[2])
    for host in range(hosts):
        for k in range(2):
            slot = moves_ref[4 * host + 2 * core + k]
            value = find(slot, pl.ds(pl.multiple_of((slot % 2) * 16, 16), 16), every)
            for side in range(2):
                send_ref[side * hosts + host, k * 16 : (k + 1) * 16, :] = value
    for k in range(2):
        live = (span_ref[k] > 0).astype(F32)
        slot = moves_ref[2 * dec + k]
        lanes = pl.ds(pl.multiple_of((slot % 2) * 128, 128), 128)
        for frame in range(2):
            lat = find(slot, slice(32 + frame * 16, 48 + frame * 16), lanes)
            x_ref[k, frame] = (lat.astype(F32) * live).astype(BF16)
        for f in range(4):
            latent = part_ref[k * 4 + f] + rest_ref[k * 4 + f] + bias_ref[...]
            x_ref[k, 2 + f] = latent.astype(BF16)


def shifted(value, step):
    line = lax.broadcasted_iota(jnp.int32, value.shape, 0)
    edge = 0 if step == 1 else value.shape[0] - 1
    moved = pltpu.roll(value, step % value.shape[0], axis=0)
    return jnp.where(line == edge, 0.0, moved)


def first_kernel(x_ref, low_ref, high_ref, weight_ref, bias_ref, first_ref, stats_ref, lat_ref, taps):
    taps[...] = jnp.zeros_like(taps)

    def fill(index, _):
        k, f = index // 6, index % 6
        wide = jnp.concatenate(
            [low_ref[k, f][:, 96:], x_ref[k, f], high_ref[k, f][:, :32]], axis=1
        ).astype(F32)
        for e, value in enumerate((shifted(wide, 1), wide, shifted(wide, -1))):
            value = value.astype(BF16)
            for r in range(10):
                taps[index, r, :, e * 48 : (e + 1) * 48] = value[:, 16 * r : 16 * r + 48]
        return 0

    lax.fori_loop(0, 12, fill, 0, unroll=12)
    for k in range(2):
        total = jnp.zeros((640, C), F32) + bias_ref[...]
        for a in range(3):
            total = total + jnp.dot(
                taps[k * 6 + a : k * 6 + a + 4].reshape(640, 256),
                weight_ref[a],
                preferred_element_type=F32,
            )
        rounded = total.astype(BF16).reshape(4, 10, 16, C)
        first_ref[k] = rounded
        own = rounded[:, 1:9].reshape(512, C).astype(F32)
        stats_ref[k : k + 1, :] = jnp.sum(own, 0, keepdims=True)
        stats_ref[2 + k : 3 + k, :] = jnp.sum(own * own, 0, keepdims=True)
        for f in range(2):
            for r in range(8):
                lat_ref[k, f, r] = x_ref[k, 4 + f][:, 16 * r : 16 * r + 16]


def group_sum(value):
    lane = lax.broadcasted_iota(jnp.int32, value.shape, 1)
    size = value.shape[1]
    for step in (1, 2, 4, 8):
        ahead = pltpu.roll(value, size - step, axis=1)
        behind = pltpu.roll(value, step, axis=1)
        value = value + jnp.where((lane // step) % 2 == 0, ahead, behind)
    return value


def spread_taps(taps, index, row, value):
    width = value.shape[1]
    for e, moved in enumerate((shifted(value, 1), value, shifted(value, -1))):
        taps[index, row, :, e * width : (e + 1) * width] = moved.astype(BF16)


def block_kernel(
    count,
    me_ref,
    span_ref,
    first_ref,
    own_ref,
    near_ref,
    far_ref,
    back_ref,
    pieces_ref,
    low_ref,
    high_ref,
    vectors_ref,
    bias_ref,
    weight_ref,
    decoded_ref,
    cache_ref,
    taps_0,
    taps_1,
    weight,
    total,
    sems,
):
    section, row = me_ref[1], me_ref[2]
    copies = [
        pltpu.make_async_copy(weight_ref.at[i], weight.at[i], sems.at[i]) for i in range(9)
    ]
    for copy in copies:
        copy.start()
    taps = (taps_0, taps_1)
    live = [(span_ref[k] > 0).astype(F32) for k in range(2)]
    sums = group_sum(own_ref[...] + near_ref[...] + far_ref[...] + back_ref[...]) / count
    mean = sums[0:2]
    scale = lax.rsqrt(sums[2:4] - mean * mean + 1e-05) * vectors_ref[1:2]
    offset = vectors_ref[2:3]
    edge = {0: (row > 0).astype(F32), 9: (row < 3).astype(F32)}

    def cached(k, f, r):
        rows = slice(k * 16, k * 16 + 16)
        if r == 0:
            pair = low_ref[0, f, rows], low_ref[1, f, rows]
        elif r == 9:
            pair = high_ref[0, f, rows], high_ref[1, f, rows]
        else:
            pair = pieces_ref[f * 8 + r - 1, rows], pieces_ref[16 + f * 8 + r - 1, rows]
        spread_taps(taps[k], f, r, jnp.concatenate(pair, axis=1).astype(F32) * live[k])

    def fresh(k, f, r, border=None):
        value = (first_ref[k, f, r].astype(F32) - mean[k : k + 1]) * scale[k : k + 1] + offset
        value = 0.5 * value * (1.0 + jnp.tanh(0.5 * value))
        if border is not None:
            value = value * border
        spread_taps(taps[k], 2 + f, r, value)

    def fill(k):
        def inner(index, _):
            fresh(k, index // 8, 1 + index % 8)
            return 0

        lax.fori_loop(0, 32, inner, 0, unroll=8)
        for f in range(4):
            for r in (0, 9):
                fresh(k, f, r, edge[r])
        for f in range(2):
            for r in range(10):
                cached(k, f, r)

    def part(k, step):
        a, b = step // 3, step % 3
        lhs = taps[k][a : a + 4, b : b + 8].reshape(512, 3 * C)
        return jnp.dot(lhs, weight[step], preferred_element_type=F32)

    start = pl.multiple_of(section * 256, 256)
    for k in range(2):
        own = first_ref[k, :, 1:9, :, pl.ds(start, 256)].astype(F32)
        total[k] = own.reshape(512, 256) + bias_ref[...]

    def finish(k):
        decoded_ref[k] = total[k].astype(BF16).reshape(4, 8, 16, 256)
        cache_ref[k] = taps[k][4:6, 1:9, :, pl.ds(C + start, 256)]

    for k in range(2):
        fill(k)
    for steps in (range(3), range(3, 9)):
        for step in steps:
            copies[step].wait()
        for k in range(2):
            value = total[k]
            for step in steps:
                value = value + part(k, step)
            total[k] = value
    for k in range(2):
        finish(k)


def beside(block):
    count = lax.axis_size("row")
    down = [(i, i + 1) for i in range(count - 1)]
    up = [(i + 1, i) for i in range(count - 1)]
    return down, up


def shards(
    hidden,
    head_weight,
    head_bias,
    lat_cache,
    mid_cache,
    moves,
    span_index,
    conv_in_weight,
    conv_in_bias,
    gn_gain,
    gn_bias,
    mid_weight,
    mid_bias,
):
    streams, frames, half_rows, half_cols, width_part = hidden.shape
    rows, cols = 2 * half_rows, 2 * half_cols
    part = conv_in_weight.shape[-1]
    section = lax.axis_index("section")
    dec = lax.axis_index("dec")
    row = lax.axis_index("row")
    bands = lax.axis_size("row")
    hosts = lax.axis_size("dec") // 2
    down, up = beside(None)
    shape = jax.ShapeDtypeStruct
    me = jnp.stack([dec, section, row]).astype(jnp.int32)

    send = call(
        pack_kernel, "pack", shape((hosts, 64, part), BF16), [VMEM, VMEM], limit=60
    )(lat_cache, mid_cache)
    spread = [[2 * j + c for j in range(hosts)] for c in range(2)]
    got = lax.all_to_all(send, "dec", 0, 0, axis_index_groups=spread)
    def whole(own):
        other = lax.ppermute(own, "section", SWAP)
        return jnp.where(
            section == 0,
            jnp.concatenate([own, other], -1),
            jnp.concatenate([other, own], -1),
        )

    in_weight = whole(conv_in_weight.transpose(0, 2, 1, 3, 4).reshape(3, 9 * CZ, part))
    in_weight = jnp.pad(in_weight, ((0, 0), (0, 256 - 9 * CZ), (0, 0)))
    vectors = whole(jnp.stack([conv_in_bias, gn_gain, gn_bias]))

    columns = head_weight.reshape(width_part, 2, 2, CZ).transpose(0, 2, 1, 3).reshape(width_part, -1)
    bias = head_bias.reshape(2, 2, CZ).transpose(1, 0, 2).reshape(1, 2, 1, 2 * CZ)
    bias = jnp.broadcast_to(bias, (half_cols, 2, half_rows, 2 * CZ)).reshape(cols, rows * CZ)
    partial = call(
        head_kernel, "head", shape((streams * frames, cols, rows * CZ), F32), [VMEM, VMEM]
    )(hidden.reshape(-1, width_part), columns)
    rest = lax.ppermute(partial, "section", SWAP)

    got, rest, in_weight, vectors = lax.optimization_barrier((got, rest, in_weight, vectors))
    twin = lax.ppermute(got, "dec", [(i, i ^ 1) for i in range(2 * hosts)])
    back, x_in = call(
        pick_kernel,
        "pick",
        (
            shape((2 * hosts, 32, part), BF16),
            shape((streams, CACHE + frames, cols, rows * CZ), BF16),
        ),
        [SMEM, SMEM, SMEM] + [VMEM] * 5,
        (VMEM, VMEM),
    )(me, moves, span_index, got, twin, partial, rest, bias)
    gather = [
        [s * 2 * hosts + 2 * j + c for s in range(2) for j in range(hosts)] for c in range(2)
    ]
    pieces = lax.all_to_all(back, ("section", "dec"), 0, 0, axis_index_groups=gather)

    low = lax.ppermute(x_in, "row", down)
    high = lax.ppermute(x_in, "row", up)
    first, stats, new_lat = call(
        first_kernel,
        "first",
        (
            shape((streams, frames, rows + 2, cols, 2 * part), BF16),
            shape((4, 2 * part), F32),
            shape((streams, CACHE, rows, cols, CZ), BF16),
        ),
        [VMEM] * 5,
        (VMEM, VMEM, VMEM),
        [pltpu.VMEM((streams * (CACHE + frames), rows + 2, cols, 256), BF16)],
    )(x_in, low, high, in_weight, vectors[0:1])
    others = [
        lax.ppermute(stats, "row", [(i, (i + shift) % bands) for i in range(bands)])
        for shift in range(1, bands)
    ]
    pieces, new_lat = lax.optimization_barrier((pieces, new_lat))
    edges = pieces.reshape(2, CACHE, rows, 32, part)
    low_mid = lax.ppermute(edges[:, :, rows - 1], "row", down)
    others, edge = lax.optimization_barrier((others, edges[:, :, 0]))
    high_mid = lax.ppermute(edge, "row", up)
    taps_weight = mid_weight.reshape(9, 3 * 2 * part, part)
    count = float(frames * rows * bands * cols * (C // GROUPS))
    decoded, new_mid = call(
        functools.partial(block_kernel, count),
        "block",
        (
            shape((streams, frames, rows, cols, part), BF16),
            shape((streams, CACHE, rows, cols, part), BF16),
        ),
        [SMEM, SMEM] + [VMEM] * 10 + [ANY],
        (VMEM, VMEM),
        [pltpu.VMEM((CACHE + frames, rows + 2, cols, 3 * 2 * part), BF16)] * 2
        + [
            pltpu.VMEM((9, 3 * 2 * part, part), BF16),
            pltpu.VMEM((streams, frames * rows * cols, part), F32),
            pltpu.SemaphoreType.DMA((9,)),
        ],
    )(
        me,
        span_index,
        first,
        stats,
        *others,
        pieces,
        low_mid,
        high_mid,
        vectors,
        mid_bias.reshape(1, part),
        taps_weight,
    )
    return (decoded, new_lat, new_mid)


def solution(mesh):
    placed = (
        P("dec", None, "row", None, "section"),
        P("section", None),
        P(),
        P("dec", None, "row", None, None),
        P("dec", None, "row", None, "section"),
        P(),
        P("dec"),
        P(None, None, None, None, "section"),
        P("section"),
        P("section"),
        P("section"),
        P(None, None, None, None, "section"),
        P("section"),
    )
    return jax.shard_map(
        shards,
        mesh=mesh,
        in_specs=placed,
        out_specs=(
            P("dec", None, "row", None, "section"),
            P("dec", None, "row", None, None),
            P("dec", None, "row", None, "section"),
        ),
        check_vma=False,
    )
```

```python
import functools

import jax
import jax.numpy as jnp
from jax import lax
from jax.experimental import pallas as pl
from jax.experimental.pallas import tpu as pltpu
from jax.sharding import PartitionSpec as P

CZ = 16
C = 512
GROUPS = 32
CACHE = 2
SWAP = [(0, 1), (1, 0)]
VMEM = pl.BlockSpec(memory_space=pltpu.VMEM)
SMEM = pl.BlockSpec(memory_space=pltpu.SMEM)
ANY = pl.BlockSpec(memory_space=pl.ANY)
F32 = jnp.float32
BF16 = jnp.bfloat16


def call(kernel, name, out_shape, in_specs, out_specs=None, scratch=(), aliases=None, limit=48):
    return pl.pallas_call(
        kernel,
        out_shape=out_shape,
        in_specs=in_specs,
        out_specs=VMEM if out_specs is None else out_specs,
        scratch_shapes=scratch,
        input_output_aliases=aliases or {},
        compiler_params=pltpu.CompilerParams(vmem_limit_bytes=limit << 20),
        name=name,
    )


def head_kernel(hidden_ref, weight_ref, out_ref):
    product = jnp.dot(hidden_ref[...], weight_ref[...], preferred_element_type=F32)
    for frame in range(out_ref.shape[0]):
        for q in range(2):
            parts = [
                product[(frame * 4 + i) * 8 : (frame * 4 + i + 1) * 8, q * 32 : (q + 1) * 32]
                for i in range(4)
            ]
            out_ref[frame, pl.ds(q, 8, stride=2), :] = jnp.concatenate(parts, axis=1)


def pack_kernel(lat_ref, mid_ref, out_ref):
    both = []
    for frame in range(2):
        rows = [lat_ref[k, frame, r] for k in range(2) for r in range(8)]
        both.append(jnp.concatenate(rows, axis=1))
    for piece in range(16):
        frame, row = divmod(piece, 8)
        for k in range(2):
            out_ref[piece, k * 16 : (k + 1) * 16, :] = mid_ref[k, frame, row]
        for frame in range(2):
            out_ref[piece, 32 + frame * 16 : 48 + frame * 16, :] = both[frame]


def pick_kernel(
    me_ref, moves_ref, span_ref, got_ref, twin_ref, part_ref, rest_ref, bias_ref, send_ref, x_ref
):
    dec = me_ref[0]
    core = dec % 2
    hosts = got_ref.shape[0]

    def find(slot, rows, lanes):
        mine = (slot // 2) % 2 == core
        source = slot // 4
        return jnp.where(mine, got_ref[source, rows, lanes], twin_ref[source, rows, lanes])

    every = slice(0, got_ref.shape[2])
    for host in range(hosts):
        for k in range(2):
            slot = moves_ref[4 * host + 2 * core + k]
            value = find(slot, pl.ds(pl.multiple_of((slot % 2) * 16, 16), 16), every)
            for side in range(2):
                send_ref[side * hosts + host, k * 16 : (k + 1) * 16, :] = value
    for k in range(2):
        live = (span_ref[k] > 0).astype(F32)
        slot = moves_ref[2 * dec + k]
        lanes = pl.ds(pl.multiple_of((slot % 2) * 128, 128), 128)
        for frame in range(2):
            lat = find(slot, slice(32 + frame * 16, 48 + frame * 16), lanes)
            x_ref[k, frame] = (lat.astype(F32) * live).astype(BF16)
        for f in range(4):
            latent = part_ref[k * 4 + f] + rest_ref[k * 4 + f] + bias_ref[...]
            x_ref[k, 2 + f] = latent.astype(BF16)


def shifted(value, step):
    line = lax.broadcasted_iota(jnp.int32, value.shape, 0)
    edge = 0 if step == 1 else value.shape[0] - 1
    moved = pltpu.roll(value, step % value.shape[0], axis=0)
    return jnp.where(line == edge, 0.0, moved)


def first_kernel(me_ref, x_ref, low_ref, high_ref, weight_ref, bias_ref, first_ref, stats_ref, lat_ref, taps):
    taps[...] = jnp.zeros_like(taps)

    above = (me_ref[2] > 0).astype(F32)
    below = (me_ref[2] < 3).astype(F32)

    def fill(index, _):
        k, f = index // 6, index % 6
        low = low_ref[k, f].astype(F32)[:, 96:] * above
        high = high_ref[k, f].astype(F32)[:, :32] * below
        wide = jnp.concatenate([low, x_ref[k, f].astype(F32), high], axis=1)
        for e, value in enumerate((shifted(wide, 1), wide, shifted(wide, -1))):
            value = value.astype(BF16)
            for r in range(10):
                taps[index, r, :, e * 48 : (e + 1) * 48] = value[:, 16 * r : 16 * r + 48]
        return 0

    lax.fori_loop(0, 12, fill, 0, unroll=12)
    for k in range(2):
        total = jnp.zeros((640, C), F32) + bias_ref[...]
        for a in range(3):
            total = total + jnp.dot(
                taps[k * 6 + a : k * 6 + a + 4].reshape(640, 256),
                weight_ref[a],
                preferred_element_type=F32,
            )
        rounded = total.astype(BF16).reshape(4, 10, 16, C)
        first_ref[k] = rounded
        own = rounded[:, 1:9].reshape(512, C).astype(F32)
        stats_ref[k : k + 1, :] = jnp.sum(own, 0, keepdims=True)
        stats_ref[2 + k : 3 + k, :] = jnp.sum(own * own, 0, keepdims=True)
        for f in range(2):
            for r in range(8):
                lat_ref[k, f, r] = x_ref[k, 4 + f][:, 16 * r : 16 * r + 16]


def group_sum(value):
    lane = lax.broadcasted_iota(jnp.int32, value.shape, 1)
    size = value.shape[1]
    for step in (1, 2, 4, 8):
        ahead = pltpu.roll(value, size - step, axis=1)
        behind = pltpu.roll(value, step, axis=1)
        value = value + jnp.where((lane // step) % 2 == 0, ahead, behind)
    return value


def spread_taps(taps, index, row, value):
    width = value.shape[1]
    for e, moved in enumerate((shifted(value, 1), value, shifted(value, -1))):
        taps[index, row, :, e * width : (e + 1) * width] = moved.astype(BF16)


def block_kernel(
    count,
    me_ref,
    span_ref,
    first_ref,
    own_ref,
    near_ref,
    far_ref,
    back_ref,
    pieces_ref,
    low_ref,
    high_ref,
    vectors_ref,
    bias_ref,
    weight_ref,
    decoded_ref,
    cache_ref,
    taps_0,
    taps_1,
    weight,
    total,
    sems,
):
    section, row = me_ref[1], me_ref[2]
    copies = [
        pltpu.make_async_copy(weight_ref.at[i], weight.at[i], sems.at[i]) for i in range(9)
    ]
    for copy in copies:
        copy.start()
    taps = (taps_0, taps_1)
    live = [(span_ref[k] > 0).astype(F32) for k in range(2)]
    sums = group_sum(own_ref[...] + near_ref[...] + far_ref[...] + back_ref[...]) / count
    mean = sums[0:2]
    scale = lax.rsqrt(sums[2:4] - mean * mean + 1e-05) * vectors_ref[1:2]
    offset = vectors_ref[2:3]
    edge = {0: (row > 0).astype(F32), 9: (row < 3).astype(F32)}

    def cached(k, f, r):
        rows = slice(k * 16, k * 16 + 16)
        if r == 0:
            pair = low_ref[0, f, rows], low_ref[1, f, rows]
        elif r == 9:
            pair = high_ref[0, f, rows], high_ref[1, f, rows]
        else:
            pair = pieces_ref[f * 8 + r - 1, rows], pieces_ref[16 + f * 8 + r - 1, rows]
        inside = live[k] * edge[r] if r in (0, 9) else live[k]
        spread_taps(taps[k], f, r, jnp.concatenate(pair, axis=1).astype(F32) * inside)

    def fresh(k, f, r, border=None):
        value = (first_ref[k, f, r].astype(F32) - mean[k : k + 1]) * scale[k : k + 1] + offset
        value = 0.5 * value * (1.0 + jnp.tanh(0.5 * value))
        if border is not None:
            value = value * border
        spread_taps(taps[k], 2 + f, r, value)

    def fill(k):
        def inner(index, _):
            fresh(k, index // 8, 1 + index % 8)
            return 0

        lax.fori_loop(0, 32, inner, 0, unroll=8)
        for f in range(4):
            for r in (0, 9):
                fresh(k, f, r, edge[r])
        for f in range(2):
            for r in range(10):
                cached(k, f, r)

    def part(k, step):
        a, b = step // 3, step % 3
        lhs = taps[k][a : a + 4, b : b + 8].reshape(512, 3 * C)
        return jnp.dot(lhs, weight[step], preferred_element_type=F32)

    start = pl.multiple_of(section * 256, 256)
    for k in range(2):
        own = first_ref[k, :, 1:9, :, pl.ds(start, 256)].astype(F32)
        total[k] = own.reshape(512, 256) + bias_ref[...]

    def finish(k):
        decoded_ref[k] = total[k].astype(BF16).reshape(4, 8, 16, 256)
        cache_ref[k] = taps[k][4:6, 1:9, :, pl.ds(C + start, 256)]

    for k in range(2):
        fill(k)
    for steps in (range(3), range(3, 9)):
        for step in steps:
            copies[step].wait()
        for k in range(2):
            value = total[k]
            for step in steps:
                value = value + part(k, step)
            total[k] = value
    for k in range(2):
        finish(k)


def beside():
    count = lax.axis_size("row")
    down = [(i, (i + 1) % count) for i in range(count)]
    up = [((i + 1) % count, i) for i in range(count)]
    return down, up


def shards(
    hidden,
    head_weight,
    head_bias,
    lat_cache,
    mid_cache,
    moves,
    span_index,
    conv_in_weight,
    conv_in_bias,
    gn_gain,
    gn_bias,
    mid_weight,
    mid_bias,
):
    streams, frames, half_rows, half_cols, width_part = hidden.shape
    rows, cols = 2 * half_rows, 2 * half_cols
    part = conv_in_weight.shape[-1]
    section = lax.axis_index("section")
    dec = lax.axis_index("dec")
    row = lax.axis_index("row")
    bands = lax.axis_size("row")
    hosts = lax.axis_size("dec") // 2
    down, up = beside()
    shape = jax.ShapeDtypeStruct
    me = jnp.stack([dec, section, row]).astype(jnp.int32)

    send = call(
        pack_kernel, "pack", shape((hosts, 64, part), BF16), [VMEM, VMEM], limit=60
    )(lat_cache, mid_cache)
    spread = [[2 * j + c for j in range(hosts)] for c in range(2)]
    got = lax.all_to_all(send, "dec", 0, 0, axis_index_groups=spread)
    def whole(own):
        other = lax.ppermute(own, "section", SWAP)
        return jnp.where(
            section == 0,
            jnp.concatenate([own, other], -1),
            jnp.concatenate([other, own], -1),
        )

    in_weight = whole(conv_in_weight.transpose(0, 2, 1, 3, 4).reshape(3, 9 * CZ, part))
    in_weight = jnp.pad(in_weight, ((0, 0), (0, 256 - 9 * CZ), (0, 0)))
    vectors = whole(jnp.stack([conv_in_bias, gn_gain, gn_bias]))

    columns = head_weight.reshape(width_part, 2, 2, CZ).transpose(0, 2, 1, 3).reshape(width_part, -1)
    bias = head_bias.reshape(2, 2, CZ).transpose(1, 0, 2).reshape(1, 2, 1, 2 * CZ)
    bias = jnp.broadcast_to(bias, (half_cols, 2, half_rows, 2 * CZ)).reshape(cols, rows * CZ)
    partial = call(
        head_kernel, "head", shape((streams * frames, cols, rows * CZ), F32), [VMEM, VMEM]
    )(hidden.reshape(-1, width_part), columns)
    rest = lax.ppermute(partial, "section", SWAP)

    got, rest, in_weight, vectors = lax.optimization_barrier((got, rest, in_weight, vectors))
    twin = lax.ppermute(got, "dec", [(i, i ^ 1) for i in range(2 * hosts)])
    back, x_in = call(
        pick_kernel,
        "pick",
        (
            shape((2 * hosts, 32, part), BF16),
            shape((streams, CACHE + frames, cols, rows * CZ), BF16),
        ),
        [SMEM, SMEM, SMEM] + [VMEM] * 5,
        (VMEM, VMEM),
    )(me, moves, span_index, got, twin, partial, rest, bias)
    gather = [
        [s * 2 * hosts + 2 * j + c for s in range(2) for j in range(hosts)] for c in range(2)
    ]
    pieces = lax.all_to_all(back, ("section", "dec"), 0, 0, axis_index_groups=gather)

    low = lax.ppermute(x_in, "row", down)
    high = lax.ppermute(x_in, "row", up)
    first, stats, new_lat = call(
        first_kernel,
        "first",
        (
            shape((streams, frames, rows + 2, cols, 2 * part), BF16),
            shape((4, 2 * part), F32),
            shape((streams, CACHE, rows, cols, CZ), BF16),
        ),
        [SMEM] + [VMEM] * 5,
        (VMEM, VMEM, VMEM),
        [pltpu.VMEM((streams * (CACHE + frames), rows + 2, cols, 256), BF16)],
    )(me, x_in, low, high, in_weight, vectors[0:1])
    others = [
        lax.ppermute(stats, "row", [(i, (i + shift) % bands) for i in range(bands)])
        for shift in range(1, bands)
    ]
    pieces, new_lat = lax.optimization_barrier((pieces, new_lat))
    edges = pieces.reshape(2, CACHE, rows, 32, part)
    low_mid = lax.ppermute(edges[:, :, rows - 1], "row", down)
    others, edge = lax.optimization_barrier((others, edges[:, :, 0]))
    high_mid = lax.ppermute(edge, "row", up)
    taps_weight = mid_weight.reshape(9, 3 * 2 * part, part)
    count = float(frames * rows * bands * cols * (C // GROUPS))
    decoded, new_mid = call(
        functools.partial(block_kernel, count),
        "block",
        (
            shape((streams, frames, rows, cols, part), BF16),
            shape((streams, CACHE, rows, cols, part), BF16),
        ),
        [SMEM, SMEM] + [VMEM] * 10 + [ANY],
        (VMEM, VMEM),
        [pltpu.VMEM((CACHE + frames, rows + 2, cols, 3 * 2 * part), BF16)] * 2
        + [
            pltpu.VMEM((9, 3 * 2 * part, part), BF16),
            pltpu.VMEM((streams, frames * rows * cols, part), F32),
            pltpu.SemaphoreType.DMA((9,)),
        ],
    )(
        me,
        span_index,
        first,
        stats,
        *others,
        pieces,
        low_mid,
        high_mid,
        vectors,
        mid_bias.reshape(1, part),
        taps_weight,
    )
    return (decoded, new_lat, new_mid)


def solution(mesh):
    placed = (
        P("dec", None, "row", None, "section"),
        P("section", None),
        P(),
        P("dec", None, "row", None, None),
        P("dec", None, "row", None, "section"),
        P(),
        P("dec"),
        P(None, None, None, None, "section"),
        P("section"),
        P("section"),
        P("section"),
        P(None, None, None, None, "section"),
        P("section"),
    )
    return jax.shard_map(
        shards,
        mesh=mesh,
        in_specs=placed,
        out_specs=(
            P("dec", None, "row", None, "section"),
            P("dec", None, "row", None, None),
            P("dec", None, "row", None, "section"),
        ),
        check_vma=False,
    )
```

```python
import functools

import jax
import jax.numpy as jnp
from jax import lax
from jax.experimental import pallas as pl
from jax.experimental.pallas import tpu as pltpu
from jax.sharding import PartitionSpec as P

CZ = 16
C = 512
GROUPS = 32
CACHE = 2
SWAP = [(0, 1), (1, 0)]
VMEM = pl.BlockSpec(memory_space=pltpu.VMEM)
SMEM = pl.BlockSpec(memory_space=pltpu.SMEM)
ANY = pl.BlockSpec(memory_space=pl.ANY)
F32 = jnp.float32
BF16 = jnp.bfloat16


def call(kernel, name, out_shape, in_specs, out_specs=None, scratch=(), aliases=None, limit=48):
    return pl.pallas_call(
        kernel,
        out_shape=out_shape,
        in_specs=in_specs,
        out_specs=VMEM if out_specs is None else out_specs,
        scratch_shapes=scratch,
        input_output_aliases=aliases or {},
        compiler_params=pltpu.CompilerParams(vmem_limit_bytes=limit << 20),
        name=name,
    )


def head_kernel(hidden_ref, weight_ref, out_ref):
    product = jnp.dot(hidden_ref[...], weight_ref[...], preferred_element_type=F32)
    for frame in range(out_ref.shape[0]):
        for q in range(2):
            parts = [
                product[(frame * 4 + i) * 8 : (frame * 4 + i + 1) * 8, q * 32 : (q + 1) * 32]
                for i in range(4)
            ]
            out_ref[frame, pl.ds(q, 8, stride=2), :] = jnp.concatenate(parts, axis=1)


def pack_kernel(lat_ref, mid_ref, out_ref, lat, spread, moved, sems):
    fetched = [pltpu.make_async_copy(lat_ref, lat, sems.at[0])] + [
        pltpu.make_async_copy(mid_ref.at[k], moved.at[:, pl.ds(k * 16, 16), :], sems.at[1 + k])
        for k in range(2)
    ]
    for copy in fetched:
        copy.start()
    fetched[0].wait()
    for frame in range(2):
        rows = [lat[k, frame, r] for k in range(2) for r in range(8)]
        both = jnp.concatenate(rows, axis=1)
        for piece in range(16):
            spread[piece, frame * 16 : (frame + 1) * 16, :] = both
    last = [pltpu.make_async_copy(spread, out_ref.at[:, pl.ds(32, 32), :], sems.at[3])]
    last[0].start()
    fetched[1].wait()
    fetched[2].wait()
    last.append(pltpu.make_async_copy(moved, out_ref.at[:, pl.ds(0, 32), :], sems.at[4]))
    last[1].start()
    for copy in last:
        copy.wait()


def pick_kernel(
    me_ref, moves_ref, span_ref, got_ref, twin_ref, part_ref, rest_ref, bias_ref, send_ref, x_ref
):
    dec = me_ref[0]
    core = dec % 2
    hosts = got_ref.shape[0]

    def find(slot, rows, lanes):
        mine = (slot // 2) % 2 == core
        source = slot // 4
        return jnp.where(mine, got_ref[source, rows, lanes], twin_ref[source, rows, lanes])

    every = slice(0, got_ref.shape[2])
    for host in range(hosts):
        for k in range(2):
            slot = moves_ref[4 * host + 2 * core + k]
            value = find(slot, pl.ds(pl.multiple_of((slot % 2) * 16, 16), 16), every)
            for side in range(2):
                send_ref[side * hosts + host, k * 16 : (k + 1) * 16, :] = value
    for k in range(2):
        live = (span_ref[k] > 0).astype(F32)
        slot = moves_ref[2 * dec + k]
        lanes = pl.ds(pl.multiple_of((slot % 2) * 128, 128), 128)
        for frame in range(2):
            lat = find(slot, slice(32 + frame * 16, 48 + frame * 16), lanes)
            x_ref[k, frame] = (lat.astype(F32) * live).astype(BF16)
        for f in range(4):
            latent = part_ref[k * 4 + f] + rest_ref[k * 4 + f] + bias_ref[...]
            x_ref[k, 2 + f] = latent.astype(BF16)


def shifted(value, step):
    line = lax.broadcasted_iota(jnp.int32, value.shape, 0)
    edge = 0 if step == 1 else value.shape[0] - 1
    moved = pltpu.roll(value, step % value.shape[0], axis=0)
    return jnp.where(line == edge, 0.0, moved)


def first_kernel(me_ref, x_ref, low_ref, high_ref, weight_ref, bias_ref, first_ref, stats_ref, lat_ref, taps):
    taps[...] = jnp.zeros_like(taps)

    above = (me_ref[2] > 0).astype(F32)
    below = (me_ref[2] < 3).astype(F32)

    def fill(index, _):
        k, f = index // 6, index % 6
        low = low_ref[k, f].astype(F32)[:, 96:] * above
        high = high_ref[k, f].astype(F32)[:, :32] * below
        wide = jnp.concatenate([low, x_ref[k, f].astype(F32), high], axis=1)
        for e, value in enumerate((shifted(wide, 1), wide, shifted(wide, -1))):
            value = value.astype(BF16)
            for r in range(10):
                taps[index, r, :, e * 48 : (e + 1) * 48] = value[:, 16 * r : 16 * r + 48]
        return 0

    lax.fori_loop(0, 12, fill, 0, unroll=12)
    for k in range(2):
        total = jnp.zeros((640, C), F32) + bias_ref[...]
        for a in range(3):
            total = total + jnp.dot(
                taps[k * 6 + a : k * 6 + a + 4].reshape(640, 256),
                weight_ref[a],
                preferred_element_type=F32,
            )
        rounded = total.astype(BF16).reshape(4, 10, 16, C)
        first_ref[k] = rounded
        own = rounded[:, 1:9].reshape(512, C).astype(F32)
        stats_ref[k : k + 1, :] = jnp.sum(own, 0, keepdims=True)
        stats_ref[2 + k : 3 + k, :] = jnp.sum(own * own, 0, keepdims=True)
        for f in range(2):
            for r in range(8):
                lat_ref[k, f, r] = x_ref[k, 4 + f][:, 16 * r : 16 * r + 16]


def group_sum(value):
    lane = lax.broadcasted_iota(jnp.int32, value.shape, 1)
    size = value.shape[1]
    for step in (1, 2, 4, 8):
        ahead = pltpu.roll(value, size - step, axis=1)
        behind = pltpu.roll(value, step, axis=1)
        value = value + jnp.where((lane // step) % 2 == 0, ahead, behind)
    return value


def spread_taps(taps, index, row, value):
    width = value.shape[1]
    for e, moved in enumerate((shifted(value, 1), value, shifted(value, -1))):
        taps[index, row, :, e * width : (e + 1) * width] = moved.astype(BF16)


def block_kernel(
    count,
    me_ref,
    span_ref,
    first_ref,
    own_ref,
    near_ref,
    far_ref,
    back_ref,
    pieces_ref,
    low_ref,
    high_ref,
    vectors_ref,
    bias_ref,
    weight_ref,
    decoded_ref,
    cache_ref,
    taps_0,
    taps_1,
    weight,
    total,
    sems,
):
    section, row = me_ref[1], me_ref[2]
    copies = [
        pltpu.make_async_copy(weight_ref.at[i], weight.at[i], sems.at[i]) for i in range(9)
    ]
    for copy in copies:
        copy.start()
    taps = (taps_0, taps_1)
    live = [(span_ref[k] > 0).astype(F32) for k in range(2)]
    sums = group_sum(own_ref[...] + near_ref[...] + far_ref[...] + back_ref[...]) / count
    mean = sums[0:2]
    scale = lax.rsqrt(sums[2:4] - mean * mean + 1e-05) * vectors_ref[1:2]
    offset = vectors_ref[2:3]
    edge = {0: (row > 0).astype(F32), 9: (row < 3).astype(F32)}

    def cached(k, f, r):
        rows = slice(k * 16, k * 16 + 16)
        if r == 0:
            pair = low_ref[0, f, rows], low_ref[1, f, rows]
        elif r == 9:
            pair = high_ref[0, f, rows], high_ref[1, f, rows]
        else:
            pair = pieces_ref[f * 8 + r - 1, rows], pieces_ref[16 + f * 8 + r - 1, rows]
        inside = live[k] * edge[r] if r in (0, 9) else live[k]
        spread_taps(taps[k], f, r, jnp.concatenate(pair, axis=1).astype(F32) * inside)

    def fresh(k, f, r, border=None):
        value = (first_ref[k, f, r].astype(F32) - mean[k : k + 1]) * scale[k : k + 1] + offset
        value = 0.5 * value * (1.0 + jnp.tanh(0.5 * value))
        if border is not None:
            value = value * border
        spread_taps(taps[k], 2 + f, r, value)

    def fill(k):
        def inner(index, _):
            fresh(k, index // 8, 1 + index % 8)
            return 0

        lax.fori_loop(0, 32, inner, 0, unroll=8)
        for f in range(4):
            for r in (0, 9):
                fresh(k, f, r, edge[r])
        for f in range(2):
            for r in range(10):
                cached(k, f, r)

    def part(k, step):
        a, b = step // 3, step % 3
        lhs = taps[k][a : a + 4, b : b + 8].reshape(512, 3 * C)
        return jnp.dot(lhs, weight[step], preferred_element_type=F32)

    start = pl.multiple_of(section * 256, 256)
    for k in range(2):
        own = first_ref[k, :, 1:9, :, pl.ds(start, 256)].astype(F32)
        total[k] = own.reshape(512, 256) + bias_ref[...]

    def finish(k):
        decoded_ref[k] = total[k].astype(BF16).reshape(4, 8, 16, 256)
        cache_ref[k] = taps[k][4:6, 1:9, :, pl.ds(C + start, 256)]

    for k in range(2):
        fill(k)
    for steps in (range(3), range(3, 9)):
        for step in steps:
            copies[step].wait()
        for k in range(2):
            value = total[k]
            for step in steps:
                value = value + part(k, step)
            total[k] = value
    for k in range(2):
        finish(k)


def beside():
    count = lax.axis_size("row")
    down = [(i, (i + 1) % count) for i in range(count)]
    up = [((i + 1) % count, i) for i in range(count)]
    return down, up


def shards(
    hidden,
    head_weight,
    head_bias,
    lat_cache,
    mid_cache,
    moves,
    span_index,
    conv_in_weight,
    conv_in_bias,
    gn_gain,
    gn_bias,
    mid_weight,
    mid_bias,
):
    streams, frames, half_rows, half_cols, width_part = hidden.shape
    rows, cols = 2 * half_rows, 2 * half_cols
    part = conv_in_weight.shape[-1]
    section = lax.axis_index("section")
    dec = lax.axis_index("dec")
    row = lax.axis_index("row")
    bands = lax.axis_size("row")
    hosts = lax.axis_size("dec") // 2
    down, up = beside()
    shape = jax.ShapeDtypeStruct
    me = jnp.stack([dec, section, row]).astype(jnp.int32)

    send = call(
        pack_kernel,
        "pack",
        shape((hosts, 64, part), BF16),
        [ANY, ANY],
        ANY,
        [
            pltpu.VMEM(lat_cache.shape, BF16),
            pltpu.VMEM((hosts, 32, part), BF16),
            pltpu.VMEM((hosts, 32, part), BF16),
            pltpu.SemaphoreType.DMA((5,)),
        ],
        limit=60,
    )(lat_cache, mid_cache.reshape(streams, hosts, cols, part))
    spread = [[2 * j + c for j in range(hosts)] for c in range(2)]
    got = lax.all_to_all(send, "dec", 0, 0, axis_index_groups=spread)
    def whole(own):
        other = lax.ppermute(own, "section", SWAP)
        return jnp.where(
            section == 0,
            jnp.concatenate([own, other], -1),
            jnp.concatenate([other, own], -1),
        )

    in_weight = whole(conv_in_weight.transpose(0, 2, 1, 3, 4).reshape(3, 9 * CZ, part))
    in_weight = jnp.pad(in_weight, ((0, 0), (0, 256 - 9 * CZ), (0, 0)))
    vectors = whole(jnp.stack([conv_in_bias, gn_gain, gn_bias]))

    columns = head_weight.reshape(width_part, 2, 2, CZ).transpose(0, 2, 1, 3).reshape(width_part, -1)
    bias = head_bias.reshape(2, 2, CZ).transpose(1, 0, 2).reshape(1, 2, 1, 2 * CZ)
    bias = jnp.broadcast_to(bias, (half_cols, 2, half_rows, 2 * CZ)).reshape(cols, rows * CZ)
    partial = call(
        head_kernel, "head", shape((streams * frames, cols, rows * CZ), F32), [VMEM, VMEM]
    )(hidden.reshape(-1, width_part), columns)
    rest = lax.ppermute(partial, "section", SWAP)

    got, rest, in_weight, vectors = lax.optimization_barrier((got, rest, in_weight, vectors))
    twin = lax.ppermute(got, "dec", [(i, i ^ 1) for i in range(2 * hosts)])
    back, x_in = call(
        pick_kernel,
        "pick",
        (
            shape((2 * hosts, 32, part), BF16),
            shape((streams, CACHE + frames, cols, rows * CZ), BF16),
        ),
        [SMEM, SMEM, SMEM] + [VMEM] * 5,
        (VMEM, VMEM),
    )(me, moves, span_index, got, twin, partial, rest, bias)
    gather = [
        [s * 2 * hosts + 2 * j + c for s in range(2) for j in range(hosts)] for c in range(2)
    ]
    pieces = lax.all_to_all(back, ("section", "dec"), 0, 0, axis_index_groups=gather)

    low = lax.ppermute(x_in, "row", down)
    high = lax.ppermute(x_in, "row", up)
    first, stats, new_lat = call(
        first_kernel,
        "first",
        (
            shape((streams, frames, rows + 2, cols, 2 * part), BF16),
            shape((4, 2 * part), F32),
            shape((streams, CACHE, rows, cols, CZ), BF16),
        ),
        [SMEM] + [VMEM] * 5,
        (VMEM, VMEM, VMEM),
        [pltpu.VMEM((streams * (CACHE + frames), rows + 2, cols, 256), BF16)],
    )(me, x_in, low, high, in_weight, vectors[0:1])
    others = [
        lax.ppermute(stats, "row", [(i, (i + shift) % bands) for i in range(bands)])
        for shift in range(1, bands)
    ]
    pieces, new_lat = lax.optimization_barrier((pieces, new_lat))
    edges = pieces.reshape(2, CACHE, rows, 32, part)
    low_mid = lax.ppermute(edges[:, :, rows - 1], "row", down)
    others, edge = lax.optimization_barrier((others, edges[:, :, 0]))
    high_mid = lax.ppermute(edge, "row", up)
    taps_weight = mid_weight.reshape(9, 3 * 2 * part, part)
    count = float(frames * rows * bands * cols * (C // GROUPS))
    decoded, new_mid = call(
        functools.partial(block_kernel, count),
        "block",
        (
            shape((streams, frames, rows, cols, part), BF16),
            shape((streams, CACHE, rows, cols, part), BF16),
        ),
        [SMEM, SMEM] + [VMEM] * 10 + [ANY],
        (VMEM, VMEM),
        [pltpu.VMEM((CACHE + frames, rows + 2, cols, 3 * 2 * part), BF16)] * 2
        + [
            pltpu.VMEM((9, 3 * 2 * part, part), BF16),
            pltpu.VMEM((streams, frames * rows * cols, part), F32),
            pltpu.SemaphoreType.DMA((9,)),
        ],
    )(
        me,
        span_index,
        first,
        stats,
        *others,
        pieces,
        low_mid,
        high_mid,
        vectors,
        mid_bias.reshape(1, part),
        taps_weight,
    )
    return (decoded, new_lat, new_mid)


def solution(mesh):
    placed = (
        P("dec", None, "row", None, "section"),
        P("section", None),
        P(),
        P("dec", None, "row", None, None),
        P("dec", None, "row", None, "section"),
        P(),
        P("dec"),
        P(None, None, None, None, "section"),
        P("section"),
        P("section"),
        P("section"),
        P(None, None, None, None, "section"),
        P("section"),
    )
    return jax.shard_map(
        shards,
        mesh=mesh,
        in_specs=placed,
        out_specs=(
            P("dec", None, "row", None, "section"),
            P("dec", None, "row", None, None),
            P("dec", None, "row", None, "section"),
        ),
        check_vma=False,
    )
```

```python
import functools

import jax
import jax.numpy as jnp
from jax import lax
from jax.experimental import pallas as pl
from jax.experimental.pallas import tpu as pltpu
from jax.sharding import PartitionSpec as P

CZ = 16
C = 512
GROUPS = 32
CACHE = 2
SWAP = [(0, 1), (1, 0)]
VMEM = pl.BlockSpec(memory_space=pltpu.VMEM)
SMEM = pl.BlockSpec(memory_space=pltpu.SMEM)
ANY = pl.BlockSpec(memory_space=pl.ANY)
F32 = jnp.float32
BF16 = jnp.bfloat16


def call(kernel, name, out_shape, in_specs, out_specs=None, scratch=(), aliases=None, limit=48):
    return pl.pallas_call(
        kernel,
        out_shape=out_shape,
        in_specs=in_specs,
        out_specs=VMEM if out_specs is None else out_specs,
        scratch_shapes=scratch,
        input_output_aliases=aliases or {},
        compiler_params=pltpu.CompilerParams(vmem_limit_bytes=limit << 20),
        name=name,
    )


def head_kernel(hidden_ref, weight_ref, out_ref):
    product = jnp.dot(hidden_ref[...], weight_ref[...], preferred_element_type=F32)
    for frame in range(out_ref.shape[0]):
        for q in range(2):
            parts = [
                product[(frame * 4 + i) * 8 : (frame * 4 + i + 1) * 8, q * 32 : (q + 1) * 32]
                for i in range(4)
            ]
            out_ref[frame, pl.ds(q, 8, stride=2), :] = jnp.concatenate(parts, axis=1)


def pack_kernel(lat_ref, mid_ref, out_ref):
    both = []
    for frame in range(2):
        rows = [lat_ref[k, frame, r] for k in range(2) for r in range(8)]
        both.append(jnp.concatenate(rows, axis=1))
    for piece in range(16):
        frame, row = divmod(piece, 8)
        for k in range(2):
            out_ref[piece, k * 16 : (k + 1) * 16, :] = mid_ref[k, frame, row]
        for frame in range(2):
            out_ref[piece, 32 + frame * 16 : 48 + frame * 16, :] = both[frame]


def pick_kernel(
    me_ref, moves_ref, span_ref, got_ref, twin_ref, part_ref, rest_ref, bias_ref, send_ref, x_ref
):
    dec = me_ref[0]
    core = dec % 2
    hosts = got_ref.shape[0]

    def find(slot, rows, lanes):
        mine = (slot // 2) % 2 == core
        source = slot // 4
        return jnp.where(mine, got_ref[source, rows, lanes], twin_ref[source, rows, lanes])

    every = slice(0, got_ref.shape[2])
    for host in range(hosts):
        for k in range(2):
            slot = moves_ref[4 * host + 2 * core + k]
            value = find(slot, pl.ds(pl.multiple_of((slot % 2) * 16, 16), 16), every)
            for side in range(2):
                send_ref[side * hosts + host, k * 16 : (k + 1) * 16, :] = value
    for k in range(2):
        live = (span_ref[k] > 0).astype(F32)
        slot = moves_ref[2 * dec + k]
        lanes = pl.ds(pl.multiple_of((slot % 2) * 128, 128), 128)
        for frame in range(2):
            lat = find(slot, slice(32 + frame * 16, 48 + frame * 16), lanes)
            x_ref[k, frame] = (lat.astype(F32) * live).astype(BF16)
        for f in range(4):
            latent = part_ref[k * 4 + f] + rest_ref[k * 4 + f] + bias_ref[...]
            x_ref[k, 2 + f] = latent.astype(BF16)


def shifted(value, step):
    line = lax.broadcasted_iota(jnp.int32, value.shape, 0)
    edge = 0 if step == 1 else value.shape[0] - 1
    moved = pltpu.roll(value, step % value.shape[0], axis=0)
    return jnp.where(line == edge, 0.0, moved)


def first_kernel(me_ref, x_ref, low_ref, high_ref, weight_ref, bias_ref, first_ref, stats_ref, lat_ref, taps):
    taps[...] = jnp.zeros_like(taps)

    above = (me_ref[2] > 0).astype(F32)
    below = (me_ref[2] < 3).astype(F32)

    def fill(index, _):
        k, f = index // 6, index % 6
        low = low_ref[k, f].astype(F32)[:, 96:] * above
        high = high_ref[k, f].astype(F32)[:, :32] * below
        wide = jnp.concatenate([low, x_ref[k, f].astype(F32), high], axis=1)
        for e, value in enumerate((shifted(wide, 1), wide, shifted(wide, -1))):
            value = value.astype(BF16)
            for r in range(10):
                taps[index, r, :, e * 48 : (e + 1) * 48] = value[:, 16 * r : 16 * r + 48]
        return 0

    lax.fori_loop(0, 12, fill, 0, unroll=12)
    for k in range(2):
        total = jnp.zeros((640, C), F32) + bias_ref[...]
        for a in range(3):
            total = total + jnp.dot(
                taps[k * 6 + a : k * 6 + a + 4].reshape(640, 256),
                weight_ref[a],
                preferred_element_type=F32,
            )
        rounded = total.astype(BF16).reshape(4, 10, 16, C)
        first_ref[k] = rounded
        own = rounded[:, 1:9].reshape(512, C).astype(F32)
        stats_ref[k : k + 1, :] = jnp.sum(own, 0, keepdims=True)
        stats_ref[2 + k : 3 + k, :] = jnp.sum(own * own, 0, keepdims=True)
        for f in range(2):
            for r in range(8):
                lat_ref[k, f, r] = x_ref[k, 4 + f][:, 16 * r : 16 * r + 16]


def group_sum(value):
    lane = lax.broadcasted_iota(jnp.int32, value.shape, 1)
    size = value.shape[1]
    for step in (1, 2, 4, 8):
        ahead = pltpu.roll(value, size - step, axis=1)
        behind = pltpu.roll(value, step, axis=1)
        value = value + jnp.where((lane // step) % 2 == 0, ahead, behind)
    return value


def spread_taps(taps, index, row, value):
    width = value.shape[1]
    for e, moved in enumerate((shifted(value, 1), value, shifted(value, -1))):
        taps[index, row, :, e * width : (e + 1) * width] = moved.astype(BF16)


def block_kernel(
    count,
    me_ref,
    span_ref,
    first_ref,
    own_ref,
    near_ref,
    far_ref,
    back_ref,
    pieces_ref,
    low_ref,
    high_ref,
    vectors_ref,
    bias_ref,
    weight_ref,
    decoded_ref,
    cache_ref,
    taps_0,
    taps_1,
    weight,
    total,
    sems,
):
    section, row = me_ref[1], me_ref[2]
    copies = [
        pltpu.make_async_copy(weight_ref.at[i], weight.at[i], sems.at[i]) for i in range(9)
    ]
    for copy in copies:
        copy.start()
    taps = (taps_0, taps_1)
    live = [(span_ref[k] > 0).astype(F32) for k in range(2)]
    sums = group_sum(own_ref[...] + near_ref[...] + far_ref[...] + back_ref[...]) / count
    mean = sums[0:2]
    scale = lax.rsqrt(sums[2:4] - mean * mean + 1e-05) * vectors_ref[1:2]
    offset = vectors_ref[2:3]
    edge = {0: (row > 0).astype(F32), 9: (row < 3).astype(F32)}

    def cached(k, f, r):
        rows = slice(k * 16, k * 16 + 16)
        if r == 0:
            pair = low_ref[0, f, rows], low_ref[1, f, rows]
        elif r == 9:
            pair = high_ref[0, f, rows], high_ref[1, f, rows]
        else:
            pair = pieces_ref[f * 8 + r - 1, rows], pieces_ref[16 + f * 8 + r - 1, rows]
        inside = live[k] * edge[r] if r in (0, 9) else live[k]
        spread_taps(taps[k], f, r, jnp.concatenate(pair, axis=1).astype(F32) * inside)

    def fresh(k, f, r, border=None):
        value = (first_ref[k, f, r].astype(F32) - mean[k : k + 1]) * scale[k : k + 1] + offset
        value = 0.5 * value * (1.0 + jnp.tanh(0.5 * value))
        if border is not None:
            value = value * border
        spread_taps(taps[k], 2 + f, r, value)

    def fill(k):
        def inner(index, _):
            fresh(k, index // 8, 1 + index % 8)
            return 0

        lax.fori_loop(0, 32, inner, 0, unroll=8)
        for f in range(4):
            for r in (0, 9):
                fresh(k, f, r, edge[r])
        for f in range(2):
            for r in range(10):
                cached(k, f, r)

    def part(k, step):
        a, b = step // 3, step % 3
        lhs = taps[k][a : a + 4, b : b + 8].reshape(512, 3 * C)
        return jnp.dot(lhs, weight[step], preferred_element_type=F32)

    start = pl.multiple_of(section * 256, 256)
    for k in range(2):
        own = first_ref[k, :, 1:9, :, pl.ds(start, 256)].astype(F32)
        total[k] = own.reshape(512, 256) + bias_ref[...]

    def finish(k):
        decoded_ref[k] = total[k].astype(BF16).reshape(4, 8, 16, 256)
        cache_ref[k] = taps[k][4:6, 1:9, :, pl.ds(C + start, 256)]

    for k in range(2):
        fill(k)
    for steps in (range(3), range(3, 9)):
        for step in steps:
            copies[step].wait()
        for k in range(2):
            value = total[k]
            for step in steps:
                value = value + part(k, step)
            total[k] = value
    for k in range(2):
        finish(k)


def beside():
    count = lax.axis_size("row")
    down = [(i, i + 1) for i in range(count - 1)]
    up = [((i + 1) % count, i) for i in range(count)]
    return down, up


def shards(
    hidden,
    head_weight,
    head_bias,
    lat_cache,
    mid_cache,
    moves,
    span_index,
    conv_in_weight,
    conv_in_bias,
    gn_gain,
    gn_bias,
    mid_weight,
    mid_bias,
):
    streams, frames, half_rows, half_cols, width_part = hidden.shape
    rows, cols = 2 * half_rows, 2 * half_cols
    part = conv_in_weight.shape[-1]
    section = lax.axis_index("section")
    dec = lax.axis_index("dec")
    row = lax.axis_index("row")
    bands = lax.axis_size("row")
    hosts = lax.axis_size("dec") // 2
    down, up = beside()
    shape = jax.ShapeDtypeStruct
    me = jnp.stack([dec, section, row]).astype(jnp.int32)

    send = call(
        pack_kernel, "pack", shape((hosts, 64, part), BF16), [VMEM, VMEM], limit=60
    )(lat_cache, mid_cache)
    spread = [[2 * j + c for j in range(hosts)] for c in range(2)]
    got = lax.all_to_all(send, "dec", 0, 0, axis_index_groups=spread)
    def whole(own):
        other = lax.ppermute(own, "section", SWAP)
        return jnp.where(
            section == 0,
            jnp.concatenate([own, other], -1),
            jnp.concatenate([other, own], -1),
        )

    in_weight = whole(conv_in_weight.transpose(0, 2, 1, 3, 4).reshape(3, 9 * CZ, part))
    in_weight = jnp.pad(in_weight, ((0, 0), (0, 256 - 9 * CZ), (0, 0)))
    vectors = whole(jnp.stack([conv_in_bias, gn_gain, gn_bias]))

    columns = head_weight.reshape(width_part, 2, 2, CZ).transpose(0, 2, 1, 3).reshape(width_part, -1)
    bias = head_bias.reshape(2, 2, CZ).transpose(1, 0, 2).reshape(1, 2, 1, 2 * CZ)
    bias = jnp.broadcast_to(bias, (half_cols, 2, half_rows, 2 * CZ)).reshape(cols, rows * CZ)
    partial = call(
        head_kernel, "head", shape((streams * frames, cols, rows * CZ), F32), [VMEM, VMEM]
    )(hidden.reshape(-1, width_part), columns)
    rest = lax.ppermute(partial, "section", SWAP)

    got, rest, in_weight, vectors = lax.optimization_barrier((got, rest, in_weight, vectors))
    twin = lax.ppermute(got, "dec", [(i, i ^ 1) for i in range(2 * hosts)])
    back, x_in = call(
        pick_kernel,
        "pick",
        (
            shape((2 * hosts, 32, part), BF16),
            shape((streams, CACHE + frames, cols, rows * CZ), BF16),
        ),
        [SMEM, SMEM, SMEM] + [VMEM] * 5,
        (VMEM, VMEM),
    )(me, moves, span_index, got, twin, partial, rest, bias)
    gather = [
        [s * 2 * hosts + 2 * j + c for s in range(2) for j in range(hosts)] for c in range(2)
    ]
    pieces = lax.all_to_all(back, ("section", "dec"), 0, 0, axis_index_groups=gather)

    low = lax.ppermute(x_in, "row", down)
    high = lax.ppermute(x_in, "row", up)
    first, stats, new_lat = call(
        first_kernel,
        "first",
        (
            shape((streams, frames, rows + 2, cols, 2 * part), BF16),
            shape((4, 2 * part), F32),
            shape((streams, CACHE, rows, cols, CZ), BF16),
        ),
        [SMEM] + [VMEM] * 5,
        (VMEM, VMEM, VMEM),
        [pltpu.VMEM((streams * (CACHE + frames), rows + 2, cols, 256), BF16)],
    )(me, x_in, low, high, in_weight, vectors[0:1])
    others = [
        lax.ppermute(stats, "row", [(i, (i + shift) % bands) for i in range(bands)])
        for shift in range(1, bands)
    ]
    pieces, new_lat = lax.optimization_barrier((pieces, new_lat))
    edges = pieces.reshape(2, CACHE, rows, 32, part)
    low_mid = lax.ppermute(edges[:, :, rows - 1], "row", down)
    others, edge = lax.optimization_barrier((others, edges[:, :, 0]))
    high_mid = lax.ppermute(edge, "row", up)
    taps_weight = mid_weight.reshape(9, 3 * 2 * part, part)
    count = float(frames * rows * bands * cols * (C // GROUPS))
    decoded, new_mid = call(
        functools.partial(block_kernel, count),
        "block",
        (
            shape((streams, frames, rows, cols, part), BF16),
            shape((streams, CACHE, rows, cols, part), BF16),
        ),
        [SMEM, SMEM] + [VMEM] * 10 + [ANY],
        (VMEM, VMEM),
        [pltpu.VMEM((CACHE + frames, rows + 2, cols, 3 * 2 * part), BF16)] * 2
        + [
            pltpu.VMEM((9, 3 * 2 * part, part), BF16),
            pltpu.VMEM((streams, frames * rows * cols, part), F32),
            pltpu.SemaphoreType.DMA((9,)),
        ],
    )(
        me,
        span_index,
        first,
        stats,
        *others,
        pieces,
        low_mid,
        high_mid,
        vectors,
        mid_bias.reshape(1, part),
        taps_weight,
    )
    return (decoded, new_lat, new_mid)


def solution(mesh):
    placed = (
        P("dec", None, "row", None, "section"),
        P("section", None),
        P(),
        P("dec", None, "row", None, None),
        P("dec", None, "row", None, "section"),
        P(),
        P("dec"),
        P(None, None, None, None, "section"),
        P("section"),
        P("section"),
        P("section"),
        P(None, None, None, None, "section"),
        P("section"),
    )
    return jax.shard_map(
        shards,
        mesh=mesh,
        in_specs=placed,
        out_specs=(
            P("dec", None, "row", None, "section"),
            P("dec", None, "row", None, None),
            P("dec", None, "row", None, "section"),
        ),
        check_vma=False,
    )
```
